32 devices in a mesh: atom: 8 (over y, x, core), mode: 4 (over z).
Axes of the slice: x: 2, y: 2, z: 4, core: 2. Of those that a mesh axis runs over, the one named last changes fastest.
Arguments:
- features: float32 [128, 8192], P(None, 'atom'), may hold values from -6 to 6
- positions: float32 [3, 8192], P(None, 'atom'), may hold values from 0 to 1, as said below
- wavevectors: int32 [3, 8192], P(None, 'mode'), may hold values from -384 to 384, as said below
- mode_filter: float32 [128, 8192], P(None, 'mode'), may hold values from -12 to 12
- radial_mix: float32 [4, 128, 128], replicated, may hold values from -0.03125 to 0.03125
- radial_rates: float32 [4], replicated, may hold values from 0.2 to 3
- neighbour_ids: int32 [64, 5], P(('atom', 'mode')), may hold values from 0 to 63, as said below
- live_counts: int32 [64], P(('atom', 'mode')), may hold values from 1 to 5, as said below
- cotangent: float32 [128, 8192], P(None, ('atom', 'mode')), may hold values from -6 to 6
Outputs:
- layer_out: float32 [128, 8192], P(None, ('atom', 'mode'))
- grad_features: float32 [128, 8192], P(None, ('atom', 'mode'))
- grad_filter: float32 [128, 8192], P(None, 'mode')
The draws below stay inside these ranges and needn't reach their ends.
Inputs may be any that keep to these rules, and one draw needn't show every extreme that they name: `positions`: row 0 of atom i lies between b / 64 and (b + 1) / 64, with b = i // 128; rows 1 and 2 lie anywhere in the range. `wavevectors`: row 0 lies between -384 and 384; rows 1 and 2 lie between -12 and 12. `neighbour_ids`: row b lists the 5 blocks (b + o) mod 64, o from -2 to 2, each once, in some order; only the first live_counts[b] slots are live. `live_counts`: some block has all 5 slots live.
All inputs are finite; a program needn't handle non-finite values.
Results may differ from the reference program's by a relative error of at most 0.00035.
Values sent between devices are 32-bit elements; how exact they have to be, the bound alone decides.
A program may use at most 128 MiB of HBM per device.

```python
import math
import jax
import jax.numpy as jnp
from jax import lax

C = 128
MODES = 8192
RADIAL = 4
BLOCK = 128
REACH = 2
ATOM_DEV = 1024
SLOTS = 5
ATOMS = 8192
NBLK = 64


def neighbour_plan(key):
    order_key = jax.random.fold_in(key, 11)
    first_key = jax.random.fold_in(key, 12)
    second_key = jax.random.fold_in(key, 13)
    shift_key = jax.random.fold_in(key, 14)
    scores = jax.random.randint(order_key, (NBLK, SLOTS), 0, 1000) * SLOTS + jnp.arange(SLOTS, dtype=jnp.int32)[None, :]
    ordering = jnp.argsort(scores, axis=1, stable=True).astype(jnp.int32)
    block_numbers = jnp.arange(NBLK, dtype=jnp.int32)
    neighbours = jnp.mod(block_numbers[:, None] + ordering - REACH, NBLK).astype(jnp.int32)
    first_draw = jax.random.randint(first_key, (NBLK,), 0, SLOTS)
    second_draw = jax.random.randint(second_key, (NBLK,), 0, SLOTS)
    shifted = jax.random.randint(shift_key, (), 0, NBLK)
    dense = jnp.mod(block_numbers + shifted, NBLK) < NBLK // 2
    counted = 1 + jnp.where(dense, jnp.maximum(first_draw, second_draw), jnp.minimum(first_draw, second_draw))
    counted = jnp.where(jnp.mod(block_numbers + shifted, NBLK) == 0, SLOTS, counted).astype(jnp.int32)
    return (neighbours, counted)


def draw_neighbour_ids(key, part):
    neighbours, counted = neighbour_plan(key)
    return neighbours


def draw_live_counts(key, part):
    neighbours, counted = neighbour_plan(key)
    return counted


def draw_wavevectors(key, part):
    long_key = jax.random.fold_in(key, 31)
    cross_key = jax.random.fold_in(key, 32)
    along = jax.random.randint(long_key, (1, MODES), -6 * NBLK, 6 * NBLK + 1)
    across = jax.random.randint(cross_key, (2, MODES), -12, 13)
    return jnp.concatenate([along, across], axis=0).astype(jnp.int32)


def draw_positions(key, part):
    inside_key = jax.random.fold_in(key, 21)
    cross_key = jax.random.fold_in(key, 22)
    inside = jax.random.uniform(inside_key, (ATOMS,), jnp.float32)
    cross = jax.random.uniform(cross_key, (2, ATOMS), jnp.float32)
    block_of = (jnp.arange(ATOMS, dtype=jnp.int32) // BLOCK).astype(jnp.float32)
    first_row = jnp.minimum((block_of + inside) / NBLK, 0.9999999)
    return jnp.concatenate([first_row[None, :], cross], axis=0).astype(jnp.float32)


def level_of(stream_key, dims, pieces, least, largest):
    factor_of = 1.0
    for dim, blocks in pieces:
        heights = jax.random.uniform(jax.random.fold_in(jax.random.fold_in(stream_key, 6), dim), (blocks,), jnp.float32, least / len(pieces), largest / len(pieces))
        factor_of = factor_of * jnp.repeat(jnp.exp(heights), dims[dim] // blocks).reshape((-1,) + (1,) * (len(dims) - 1 - dim))
    return factor_of


def bell_draw(key, dims, scale, bound, cuts=(), held_as=jnp.bfloat16):
    array = scale * jax.random.normal(key, dims, jnp.float32)
    if cuts:
        array = array * level_of(key, dims, cuts, -0.22, 0.18)
    return jnp.clip(array, -bound, bound).astype(held_as)


def setup_inputs(seed: int = 0) -> dict:
    key_list = jax.random.split(jax.random.key(seed), 10)
    return {
        "features": bell_draw(key_list[0], (C, ATOMS), 1.0, 6.0, ((1, 8),), jnp.float32),
        "positions": draw_positions(jax.random.fold_in(key_list[9], 71), 0),
        "wavevectors": draw_wavevectors(jax.random.fold_in(key_list[9], 71), 0),
        "mode_filter": bell_draw(key_list[3], (C, MODES), 2.0, 12.0, ((1, 4),), jnp.float32),
        "radial_mix": bell_draw(key_list[4], (RADIAL, C, C), (RADIAL * C * 64) ** -0.5, 0.03125, (), jnp.float32),
        "radial_rates": jnp.clip(jnp.exp(jax.random.uniform(key_list[5], (RADIAL,), jnp.float32, math.log(0.2), math.log(3.0))), 0.2, 3.0),
        "neighbour_ids": draw_neighbour_ids(jax.random.fold_in(key_list[9], 71), 0),
        "live_counts": draw_live_counts(jax.random.fold_in(key_list[9], 71), 0),
        "cotangent": bell_draw(key_list[8], (C, ATOMS), 1.0, 6.0, ((1, 32),), jnp.float32),
    }


def wave_tables(coords, wavevectors):
    wave_float = wavevectors.astype(jnp.float32)
    phases = 2.0 * jnp.pi * (coords[0][:, None] * wave_float[0][None, :] + coords[1][:, None] * wave_float[1][None, :] + coords[2][:, None] * wave_float[2][None, :])
    return jnp.cos(phases), jnp.sin(phases)


def pair_weights(own_coords, other_coords, radial_rates, total_blocks, live_mask):
    lengths = (total_blocks / jnp.pi, 2.0 / jnp.pi, 2.0 / jnp.pi)
    squared = None
    for axis_number in range(3):
        difference = own_coords[axis_number][:, None, :, None] - other_coords[axis_number][:, :, None, :]
        term = (lengths[axis_number] * jnp.sin(jnp.pi * difference)) ** 2
        squared = term if squared is None else squared + term
    return jnp.exp(-radial_rates[:, None, None, None, None] * squared[None]) * live_mask[None, :, :, None, None]


def matmul_exact(left, right):
    return jnp.dot(left, right, precision=lax.Precision.HIGHEST, preferred_element_type=jnp.float32)


def general_exact(left, right):
    return lax.dot_general(left, right, (((1,), (1,)), ((), ())), precision=lax.Precision.HIGHEST, preferred_element_type=jnp.float32)


def reference(features, positions, wavevectors, mode_filter, radial_mix, radial_rates, neighbour_ids, live_counts, cotangent):
    channels, atoms_total = features.shape
    inverse_count = 1.0 / atoms_total
    group_rows = ATOM_DEV
    group_count = atoms_total // group_rows
    feat_groups = features.reshape(channels, group_count, group_rows).transpose(1, 0, 2)
    cot_groups = cotangent.reshape(channels, group_count, group_rows).transpose(1, 0, 2)
    pos_groups = positions.reshape(3, group_count, group_rows).transpose(1, 0, 2)

    def accumulate(totals, inputs):
        feat_part, cot_part, pos_part = inputs
        cosines, sines = wave_tables(pos_part, wavevectors)
        return (totals[0] + matmul_exact(feat_part, cosines), totals[1] + matmul_exact(feat_part, sines), totals[2] + matmul_exact(cot_part, cosines), totals[3] + matmul_exact(cot_part, sines)), None

    zero_sums = jnp.zeros((channels, MODES), jnp.float32)
    sums, _ = lax.scan(accumulate, (zero_sums, zero_sums, zero_sums, zero_sums), (feat_groups, cot_groups, pos_groups))
    cos_sums, sin_sums, cot_cos, cot_sin = sums
    filt_cos = mode_filter * cos_sums * inverse_count
    filt_sin = mode_filter * sin_sums * inverse_count
    back_cos = mode_filter * cot_cos * inverse_count
    back_sin = mode_filter * cot_sin * inverse_count
    grad_filter = (cos_sums * cot_cos + sin_sums * cot_sin) * inverse_count

    def give_back(pos_part):
        cosines, sines = wave_tables(pos_part, wavevectors)
        return (general_exact(filt_cos, cosines) + general_exact(filt_sin, sines), general_exact(back_cos, cosines) + general_exact(back_sin, sines))

    long_groups, back_groups = lax.map(give_back, pos_groups)
    long_range = long_groups.transpose(1, 0, 2).reshape(channels, atoms_total)
    back_long = back_groups.transpose(1, 0, 2).reshape(channels, atoms_total)

    block_count = atoms_total // BLOCK
    blocks = features.reshape(channels, block_count, BLOCK)
    coord_blocks = positions.reshape(3, block_count, BLOCK)
    flat_ids = neighbour_ids.reshape(-1).astype(jnp.int32)
    nearby_feat = jnp.take(blocks, flat_ids, axis=1).reshape(channels, block_count, SLOTS, BLOCK)
    nearby_coord = jnp.take(coord_blocks, flat_ids, axis=1).reshape(3, block_count, SLOTS, BLOCK)
    live_mask = (jnp.arange(SLOTS, dtype=jnp.int32)[None, :] < live_counts[:, None]).astype(jnp.float32)
    weights = pair_weights(coord_blocks, nearby_coord, radial_rates, block_count, live_mask)
    gathered = jnp.einsum('cosj,rosij->rcoi', nearby_feat, weights, precision=lax.Precision.HIGHEST)
    short_range = jnp.einsum('rdc,rdoi->coi', radial_mix, gathered, precision=lax.Precision.HIGHEST).reshape(channels, atoms_total)
    layer_out = features + long_range + short_range
    back_mix = jnp.einsum('rdc,coi->rdoi', radial_mix, cotangent.reshape(channels, block_count, BLOCK), precision=lax.Precision.HIGHEST)
    contribution = jnp.einsum('rosij,rdoi->dosj', weights, back_mix, precision=lax.Precision.HIGHEST)
    back_short = jnp.zeros((channels, block_count, BLOCK), jnp.float32).at[:, flat_ids, :].add(contribution.reshape(channels, block_count * SLOTS, BLOCK))
    grad_features = cotangent + back_long + back_short.reshape(channels, atoms_total)
    return layer_out, grad_features, grad_filter
```

```python
import functools

import jax
import jax.numpy as jnp
from jax import lax
from jax.experimental import pallas as pl
from jax.experimental.pallas import tpu as pltpu
from jax.sharding import PartitionSpec as P

BLOCK = 128
REACH = 2
SLOTS = 5
ROWS = 16
VMEM_LIMIT = 56 * 1024 * 1024

SIN_ROOT = (4.442882919124344, -7.308245686508998, 3.606354218431858, -0.8461116503680876, 0.10982451641509068)
COS_ROOT = (1.4142134962552282, -6.978850948563766, 5.73946037690631, -1.8835579059813616, 0.31068802751622054)
SIN_HALF = (3.141592640130707, -5.167710083507862, 2.550077523214134, -0.5982912856178576, 0.0776576603009221)


def horner(coefs, z):
    value = coefs[-1]
    for coef in coefs[-2::-1]:
        value = value * z + coef
    return value


def split(x):
    high = x.astype(jnp.bfloat16)
    return high, (x - high.astype(jnp.float32)).astype(jnp.bfloat16)


def dot3(left, right, dims):
    def one(a, b):
        return lax.dot_general(a, b, (dims, ((), ())), preferred_element_type=jnp.float32)

    return one(left[0], right[0]) + (one(left[0], right[1]) + one(left[1], right[0]))


NN = ((1,), (0,))
NT = ((1,), (1,))
TN = ((0,), (0,))


def forward_kernel(feat_ref, cot_ref, pos_ref, wave_ref, sums_ref, ch_ref, cl_ref, sh_ref, sl_ref, fh, fl):
    channels = feat_ref.shape[0]

    @pl.when(pl.program_id(0) == 0)
    def _():
        for n, ref in enumerate((feat_ref, cot_ref)):
            high, low = split(ref[...])
            fh[n * channels : (n + 1) * channels, :] = high
            fl[n * channels : (n + 1) * channels, :] = low

    tile = wave_ref.shape[0]

    @pl.loop(0, tile // ROWS)
    def _(step):
        rows = pl.ds(pl.multiple_of(step * ROWS, ROWS), ROWS)
        wave = wave_ref[rows, :]
        turns = (
            wave[:, 0:1] * pos_ref[0:1, :] + wave[:, 1:2] * pos_ref[1:2, :] + wave[:, 2:3] * pos_ref[2:3, :]
        )
        r = turns - jnp.round(turns)
        z = r * r
        s = r * horner(SIN_ROOT, z)
        c = horner(COS_ROOT, z)
        ch_ref[rows, :], cl_ref[rows, :] = split(1.0 - s * s)
        sh_ref[rows, :], sl_ref[rows, :] = split(s * c)

    left = (fh[...], fl[...])
    sums_ref[0, : 2 * channels, :] = dot3(left, (ch_ref[...], cl_ref[...]), NT)
    sums_ref[0, 2 * channels :, :] = dot3(left, (sh_ref[...], sl_ref[...]), NT)


def forward_call(features, cotangent, positions, waves, tiles):
    channels, atoms = features.shape
    modes = waves.shape[0]
    tile = modes // tiles
    table = jax.ShapeDtypeStruct((modes, atoms), jnp.bfloat16)
    whole = lambda i: (0, 0)
    return pl.pallas_call(
        forward_kernel,
        grid=(tiles,),
        out_shape=(jax.ShapeDtypeStruct((tiles, 4 * channels, tile), jnp.float32),) + (table,) * 4,
        in_specs=[
            pl.BlockSpec((channels, atoms), whole),
            pl.BlockSpec((channels, atoms), whole),
            pl.BlockSpec(positions.shape, whole),
            pl.BlockSpec((tile, waves.shape[1]), lambda i: (i, 0)),
        ],
        out_specs=[pl.BlockSpec((1, 4 * channels, tile), lambda i: (i, 0, 0))]
        + [pl.BlockSpec((tile, atoms), lambda i: (i, 0))] * 4,
        scratch_shapes=[pltpu.VMEM((2 * channels, atoms), jnp.bfloat16)] * 2,
        compiler_params=pltpu.CompilerParams(vmem_limit_bytes=VMEM_LIMIT),
        cost_estimate=pl.CostEstimate(flops=24 * channels * atoms * modes, bytes_accessed=8 * atoms * modes, transcendentals=0),
        name="forward_sums",
    )(features, cotangent, positions, waves)


def backward_kernel(filt_ref, ch_ref, cl_ref, sh_ref, sl_ref, out_ref):
    half = out_ref.shape[1]
    width = out_ref.shape[2]

    @pl.when(pl.program_id(0) == 0)
    def _():
        out_ref[...] = jnp.zeros_like(out_ref)

    cos_left = split(filt_ref[0, :half, :])
    sin_left = split(filt_ref[0, half : 2 * half, :])
    for q in range(out_ref.shape[0]):
        cols = slice(q * width, (q + 1) * width)
        out_ref[q] += dot3(cos_left, (ch_ref[:, cols], cl_ref[:, cols]), NN) + dot3(
            sin_left, (sh_ref[:, cols], sl_ref[:, cols]), NN
        )


def backward_call(filtered, tables, parts):
    tiles, rows, tile = filtered.shape
    channels = rows // 5
    modes, atoms = tables[0].shape
    return pl.pallas_call(
        backward_kernel,
        grid=(tiles,),
        out_shape=jax.ShapeDtypeStruct((parts, 2 * channels, atoms // parts), jnp.float32),
        in_specs=[pl.BlockSpec((1, rows, tile), lambda i: (i, 0, 0))]
        + [pl.BlockSpec((tile, atoms), lambda i: (i, 0))] * 4,
        out_specs=pl.BlockSpec((parts, 2 * channels, atoms // parts), lambda i: (0, 0, 0)),
        compiler_params=pltpu.CompilerParams(vmem_limit_bytes=VMEM_LIMIT),
        cost_estimate=pl.CostEstimate(flops=24 * channels * atoms * modes, bytes_accessed=8 * atoms * modes, transcendentals=0),
        name="backward_sums",
    )(filtered, *tables)


def short_kernel(total_blocks, near_ref, far_ref, col_ref, row_ref, mix_ref, rate_ref, short_ref, back_ref):
    window = near_ref.shape[1]
    own = row_ref.shape[1]
    lengths = (total_blocks / jnp.pi, 2.0 / jnp.pi, 2.0 / jnp.pi)
    near = split(near_ref[...])
    far = split(far_ref[...])
    reach = window - own + BLOCK
    slots = reach // BLOCK
    for b in range(own // BLOCK):
        mine = slice(b * BLOCK, (b + 1) * BLOCK)
        around = slice(b * BLOCK, b * BLOCK + reach)
        squares = []
        for t in range(slots):
            rows = slice((b + t) * BLOCK, (b + t + 1) * BLOCK)
            total = None
            for d in range(3):
                turn = row_ref[d : d + 1, mine] - col_ref[rows, d : d + 1]
                r = turn - jnp.round(turn)
                term = (lengths[d] * (r * horner(SIN_HALF, r * r))) ** 2
                total = term if total is None else total + term
            squares.append(total)
        short = None
        for n in range(mix_ref.shape[0]):
            rate = rate_ref[n]
            ahead, behind = [], []
            for t in range(slots):
                rows = slice((b + t) * BLOCK, (b + t + 1) * BLOCK)
                weight = jnp.exp(-rate * squares[t])
                ahead.append(weight * row_ref[8 + t : 9 + t, mine])
                behind.append(weight * col_ref[rows, 8 + slots - 1 - t : 8 + slots - t])
            gathered = dot3([x[:, around] for x in near], split(jnp.concatenate(ahead, axis=0)), NN)
            returned = dot3([x[:, around] for x in far], split(jnp.concatenate(behind, axis=0)), NN)
            mix = split(mix_ref[n])
            forth = dot3(mix, split(gathered), TN)
            back = dot3(mix, split(returned), NN)
            short = (forth, back) if short is None else (short[0] + forth, short[1] + back)
        short_ref[:, mine] = short[0]
        back_ref[:, mine] = short[1]


def short_call(near, far, col, row, radial_mix, radial_rates, total_blocks):
    channels, own = near.shape[0], row.shape[1]
    vmem = pl.BlockSpec(memory_space=pltpu.VMEM)
    return pl.pallas_call(
        functools.partial(short_kernel, total_blocks),
        out_shape=(jax.ShapeDtypeStruct((channels, own), jnp.float32),) * 2,
        in_specs=[vmem] * 5 + [pl.BlockSpec(memory_space=pltpu.SMEM)],
        out_specs=[vmem] * 2,
        compiler_params=pltpu.CompilerParams(vmem_limit_bytes=VMEM_LIMIT),
        cost_estimate=pl.CostEstimate(flops=6_000_000_000, bytes_accessed=4_000_000, transcendentals=0),
        name="short_range",
    )(near, far, col, row, radial_mix, radial_rates)


def per_device(features, positions, wavevectors, mode_filter, radial_mix, radial_rates, neighbour_ids, live_counts, cotangent):
    channels, shard_atoms = features.shape
    atom_devices = lax.axis_size("atom")
    mode_devices = lax.axis_size("mode")
    total_atoms = shard_atoms * atom_devices
    inverse_count = 1.0 / total_atoms
    total_blocks = total_atoms // BLOCK
    owned_blocks = neighbour_ids.shape[0]
    owned_rows = owned_blocks * BLOCK
    reach_rows = REACH * BLOCK
    mode_index = lax.axis_index("mode")
    atom_index = lax.axis_index("atom")

    first_own = (atom_index * mode_devices + mode_index) * owned_blocks
    offsets = jnp.mod(
        neighbour_ids - (first_own + jnp.arange(owned_blocks, dtype=jnp.int32))[:, None] + REACH, total_blocks
    )
    live = jnp.arange(SLOTS, dtype=jnp.int32)[None, :] < live_counts[:, None]
    masks = jnp.sum(
        jnp.where(live[:, :, None] & (offsets[:, :, None] == jnp.arange(8, dtype=jnp.int32)), 1.0, 0.0), axis=1
    )
    mask_rows = jnp.repeat(masks.T, BLOCK, axis=1)
    portion = lax.all_gather(jnp.concatenate([cotangent, mask_rows], axis=0), "mode", axis=1, tiled=True)

    stacked = jnp.concatenate([features, portion, jnp.pad(positions, ((0, 5), (0, 0)))], axis=0)
    ring = [(i, (i + 1) % atom_devices) for i in range(atom_devices)]
    before = lax.ppermute(stacked[:, -reach_rows:], "atom", ring)
    after = lax.ppermute(stacked[:, :reach_rows], "atom", [(b, a) for a, b in ring])

    waves = wavevectors.astype(jnp.float32).T
    sums, *tables = forward_call(features, portion[:channels], positions, waves, atom_devices)
    share = lax.psum_scatter(sums, "atom", scatter_dimension=0, tiled=False)

    extended = jnp.concatenate([before, stacked, after], axis=1)
    near_all = lax.dynamic_slice_in_dim(extended, mode_index * owned_rows, owned_rows + 2 * reach_rows, 1)
    small = jnp.concatenate([near_all[2 * channels + 8 :], near_all[2 * channels : 2 * channels + 8]], axis=0)
    short_own, back_short = short_call(
        near_all[:channels],
        near_all[channels : 2 * channels],
        small.T,
        small[:, reach_rows:-reach_rows],
        radial_mix,
        radial_rates,
        total_blocks,
    )

    width = mode_filter.shape[1] // atom_devices
    filter_share = lax.dynamic_slice_in_dim(mode_filter, atom_index * width, width, 1) * inverse_count
    quads = share.reshape(4, channels, width)
    grad_share = (quads[0] * quads[1] + quads[2] * quads[3]) * inverse_count
    filtered = jnp.concatenate([(filter_share[None] * quads).reshape(4 * channels, width), grad_share], axis=0)
    gathered = lax.all_gather(filtered, "atom", axis=0, tiled=False)
    grad_filter = gathered[:, 4 * channels :, :].transpose(1, 0, 2).reshape(channels, -1)

    parts = backward_call(gathered, tables, mode_devices)
    own = lax.psum_scatter(parts, "mode", scatter_dimension=0, tiled=False)
    own_feat = lax.dynamic_slice_in_dim(features, mode_index * owned_rows, owned_rows, 1)
    return (
        own_feat + own[:channels] + short_own,
        cotangent + own[channels:] + back_short,
        grad_filter,
    )


def solution(mesh):
    in_specs = (
        P(None, "atom"),
        P(None, "atom"),
        P(None, "mode"),
        P(None, "mode"),
        P(),
        P(),
        P(("atom", "mode"), None),
        P(("atom", "mode")),
        P(None, ("atom", "mode")),
    )
    out_specs = (P(None, ("atom", "mode")), P(None, ("atom", "mode")), P(None, "mode"))
    return jax.shard_map(per_device, mesh=mesh, in_specs=in_specs, out_specs=out_specs, check_vma=False)
```

```python
import functools

import jax
import jax.numpy as jnp
from jax import lax
from jax.experimental import pallas as pl
from jax.experimental.pallas import tpu as pltpu
from jax.sharding import PartitionSpec as P

BLOCK = 128
REACH = 2
SLOTS = 5
ROWS = 16
VMEM_LIMIT = 56 * 1024 * 1024

SIN_ROOT = (4.442882919124344, -7.308245686508998, 3.606354218431858, -0.8461116503680876, 0.10982451641509068)
COS_ROOT = (1.4142134962552282, -6.978850948563766, 5.73946037690631, -1.8835579059813616, 0.31068802751622054)
SIN_HALF = (3.141592640130707, -5.167710083507862, 2.550077523214134, -0.5982912856178576, 0.0776576603009221)


def horner(coefs, z):
    value = coefs[-1]
    for coef in coefs[-2::-1]:
        value = value * z + coef
    return value


def split(x):
    high = x.astype(jnp.bfloat16)
    return high, (x - high.astype(jnp.float32)).astype(jnp.bfloat16)


def dot3(left, right, dims):
    def one(a, b):
        return lax.dot_general(a, b, (dims, ((), ())), preferred_element_type=jnp.float32)

    return one(left[0], right[0]) + (one(left[0], right[1]) + one(left[1], right[0]))


NN = ((1,), (0,))
NT = ((1,), (1,))
TN = ((0,), (0,))


def bits_of(count):
    return [1 << k for k in range(count.bit_length() - 1)]


def spectral_kernel(
    n, m, scale,
    feat_ref, cot_ref, pos_ref, wave_ref, filt_ref,
    out_ref, grad_ref,
    fh, fl, cots, ch, cl, sh, sl, held, pair_in, halves_in, full,
    z_send, z_recv, c_send, c_recv, r_send, r_recv, g_send, g_recv, k_send, k_recv,
):
    atom = lax.axis_index("atom")
    mode = lax.axis_index("mode")
    channels, atoms = feat_ref.shape
    part = channels // 2
    own = cot_ref.shape[1]
    tile = ch.shape[1]
    bits = bits_of(n)
    core, rest = bits[0], bits[1:]
    orders = (rest, rest[::-1])
    signs = {bit: 1 - 2 * ((atom // bit) % 2) for bit in bits}

    def at(e):
        place = atom
        for bit in bits:
            if e & bit:
                place = place + signs[bit] * bit
        return place

    def share_of(ref, e, h):
        rows = pl.ds(h * part, part)
        if len(ref.shape) == 3:
            return ref.at[at(e), rows, :]
        return ref.at[rows, pl.ds(pl.multiple_of(at(e) * tile, tile), tile)]

    def remote(src, dst, send, recv, where):
        return pltpu.make_async_remote_copy(
            src_ref=src, dst_ref=dst, send_sem=send, recv_sem=recv, device_id=where, device_id_type=pl.DeviceIdType.MESH
        )

    peers = [{"atom": at(bit)} for bit in bits] + [{"mode": lax.rem(mode + r, m)} for r in range(1, m)]
    barrier = pltpu.get_barrier_semaphore()
    for peer in peers:
        pl.semaphore_signal(barrier, inc=1, device_id=peer, device_id_type=pl.DeviceIdType.MESH)
    pl.semaphore_wait(barrier, len(peers))

    gathers = []
    for r in range(1, m):
        gathers.append(remote(cot_ref, cots.at[r - 1], z_send.at[r - 1], z_recv.at[r - 1], {"mode": lax.rem(mode + r, m)}))
        gathers[-1].start()

    def trig(e):
        first = at(e) * tile

        @pl.loop(0, tile // ROWS)
        def _(step):
            rows = pl.ds(pl.multiple_of(step * ROWS, ROWS), ROWS)
            wave = wave_ref[pl.ds(pl.multiple_of(first + step * ROWS, ROWS), ROWS), :]
            turns = (
                wave[:, 0:1] * pos_ref[0:1, :] + wave[:, 1:2] * pos_ref[1:2, :] + wave[:, 2:3] * pos_ref[2:3, :]
            )
            r = turns - jnp.round(turns)
            z = r * r
            s = r * horner(SIN_ROOT, z)
            c = horner(COS_ROOT, z)
            ch[e, rows, :], cl[e, rows, :] = split(1.0 - s * s)
            sh[e, rows, :], sl[e, rows, :] = split(s * c)

    def place(rows_from, value, cols):
        high, low = split(value)
        for h in range(2):
            rows = slice(h * channels + rows_from, h * channels + rows_from + part)
            fh[rows, cols] = high[h * part : (h + 1) * part]
            fl[rows, cols] = low[h * part : (h + 1) * part]

    place(0, feat_ref[...], slice(None))
    place(part, cot_ref[...], pl.ds(pl.multiple_of(mode * own, own), own))

    evens = [e for e in range(n - 2, -1, -2)]
    sequence = [t for e in evens for t in (e + 1, e)]
    ahead = n // 2
    for e in sequence[:ahead]:
        trig(e)
    for r in range(1, m):
        gathers[r - 1].wait_recv()
        sender = lax.rem(mode - r + m, m)
        place(part, cots[r - 1], pl.ds(pl.multiple_of(sender * own, own), own))

    sent = list(gathers)

    def sums(e):
        left = (fh[...], fl[...])
        for k, (high, low) in enumerate(((ch, cl), (sh, sl))):
            result = dot3(left, (high[e], low[e]), NT)
            held[e, 0, k] = result[:channels]
            held[e, 1, k] = result[channels:]

    landing = {}
    for h in range(2):
        live = evens
        for s, bit in enumerate(orders[h]):
            for e in live:
                if not e & bit:
                    landing[h, s, e] = len(landing)
            live = [e for e in live if not e & bit]

    def stage_copy(h, s, e):
        bit = orders[h][s]
        slot = landing[h, s, e & ~bit]
        return remote(held.at[e | bit, h], halves_in.at[slot], r_send.at[slot], r_recv.at[slot], {"atom": at(bit)})

    def advance(h, e):
        for s, bit in enumerate(orders[h]):
            copy = stage_copy(h, s, e)
            if e & bit:
                copy.start()
                sent.append(copy)
                return
            copy.wait_recv()
            held[e, h] += halves_in[landing[h, s, e]]

    for number, e in enumerate(evens):
        if 2 * number >= ahead:
            trig(e + 1)
        sums(e + 1)
        across = remote(held.at[e + 1], pair_in.at[e // 2], c_send.at[e // 2], c_recv.at[e // 2], {"atom": at(core)})
        across.start()
        sent.append(across)
        if 2 * number + 1 >= ahead:
            trig(e)
        sums(e)
        across.wait_recv()
        held[e] += pair_in[e // 2]
        for h in range(2):
            advance(h, e)

    back = [order[::-1] for order in orders]

    def box(h, e):
        return held.at[0, h] if e == 0 else full.at[e, h]

    def half_copy(h, e, bit):
        slot = h * n + (e | bit)
        return remote(box(h, e), full.at[e | bit, h], g_send.at[slot], g_recv.at[slot], {"atom": at(bit)})

    def last_of(h, e):
        return max(p for p, bit in enumerate(back[h]) if e & bit)

    def forward(h, e, first):
        for bit in back[h][first:]:
            copy = half_copy(h, e, bit)
            copy.start()
            sent.append(copy)

    def core_copy(e):
        source = held.at[0] if e == 0 else full.at[e]
        return remote(source, full.at[e | core], k_send.at[e // 2], k_recv.at[e // 2], {"atom": at(core)})

    def arrive(h, e):
        p = last_of(h, e)
        half_copy(h, e & ~back[h][p], back[h][p]).wait_recv()
        forward(h, e, p + 1)

    def give_back(e, first):
        value = held if e == 0 else full
        left = []
        for k in range(2):
            rows = []
            for h in range(2):
                factor = share_of(filt_ref, e, h)[...] * scale
                rows += [factor * value[e, h, k, :part], factor * value[e, h, k, part:]]
            left.append(split(jnp.concatenate(rows, axis=0)))
        for h in range(2):
            share_of(grad_ref, e, h)[...] = (
                value[e, h, 0, :part] * value[e, h, 0, part:] + value[e, h, 1, :part] * value[e, h, 1, part:]
            ) * scale
        for q in range(m):
            chunk = slice(q * own, (q + 1) * own)
            total = dot3(left[0], (ch[e, :, chunk], cl[e, :, chunk]), NN) + dot3(
                left[1], (sh[e, :, chunk], sl[e, :, chunk]), NN
            )
            if first:
                out_ref[q] = total
            else:
                out_ref[q] += total

    for stage in range(len(rest)):
        for h in range(2):
            copy = half_copy(h, 0, back[h][stage])
            copy.start()
            sent.append(copy)
    copy = core_copy(0)
    copy.start()
    sent.append(copy)
    give_back(0, True)

    arrivals = sorted(
        ((h, e) for e in evens if e for h in range(2)), key=lambda x: (bin(x[1]).count("1"), last_of(*x), x[1])
    )
    waiting = 0
    arrived = set()
    for h, e in arrivals:
        arrive(h, e)
        arrived.add((h, e))
        if (1 - h, e) in arrived:
            copy = core_copy(e)
            copy.start()
            sent.append(copy)
            core_copy(waiting).wait_recv()
            give_back(waiting | core, False)
            give_back(e, False)
            waiting = e
    core_copy(waiting).wait_recv()
    give_back(waiting | core, False)
    for copy in sent:
        copy.wait_send()


def spectral_call(features, cotangent, positions, waves, mode_filter, n, m, scale):
    channels, atoms = features.shape
    modes = waves.shape[0]
    tile = modes // n
    own = cotangent.shape[1]
    vmem = pl.BlockSpec(memory_space=pltpu.VMEM)
    dma = pltpu.SemaphoreType.DMA
    table = pltpu.VMEM((n, tile, atoms), jnp.bfloat16)
    slots = 2 * (n // 2 - 1)
    return pl.pallas_call(
        functools.partial(spectral_kernel, n, m, scale),
        out_shape=(
            jax.ShapeDtypeStruct((m, 2 * channels, own), jnp.float32),
            jax.ShapeDtypeStruct(mode_filter.shape, jnp.float32),
        ),
        in_specs=[vmem] * 5,
        out_specs=[vmem] * 2,
        scratch_shapes=[
            pltpu.VMEM((2 * channels, atoms), jnp.bfloat16),
            pltpu.VMEM((2 * channels, atoms), jnp.bfloat16),
            pltpu.VMEM((m - 1, channels, own), jnp.float32),
            table, table, table, table,
            pltpu.VMEM((n, 2, 2, channels, tile), jnp.float32),
            pltpu.VMEM((n // 2, 2, 2, channels, tile), jnp.float32),
            pltpu.VMEM((slots, 2, channels, tile), jnp.float32),
            pltpu.VMEM((n, 2, 2, channels, tile), jnp.float32),
            dma((m - 1,)), dma((m - 1,)),
            dma((n // 2,)), dma((n // 2,)),
            dma((slots,)), dma((slots,)),
            dma((2 * n,)), dma((2 * n,)),
            dma((n // 2,)), dma((n // 2,)),
        ],
        compiler_params=pltpu.CompilerParams(vmem_limit_bytes=VMEM_LIMIT, collective_id=0, has_side_effects=True),
        cost_estimate=pl.CostEstimate(flops=60 * channels * atoms * modes, bytes_accessed=8 * atoms * modes, transcendentals=0),
        name="spectral",
    )(features, cotangent, positions, waves, mode_filter)


def short_kernel(total_blocks, near_ref, far_ref, col_ref, row_ref, mix_ref, rate_ref, short_ref, back_ref):
    window = near_ref.shape[1]
    own = row_ref.shape[1]
    lengths = (total_blocks / jnp.pi, 2.0 / jnp.pi, 2.0 / jnp.pi)
    near = split(near_ref[...])
    far = split(far_ref[...])
    reach = window - own + BLOCK
    slots = reach // BLOCK
    for b in range(own // BLOCK):
        mine = slice(b * BLOCK, (b + 1) * BLOCK)
        around = slice(b * BLOCK, b * BLOCK + reach)
        squares = []
        for t in range(slots):
            rows = slice((b + t) * BLOCK, (b + t + 1) * BLOCK)
            total = None
            for d in range(3):
                turn = row_ref[d : d + 1, mine] - col_ref[rows, d : d + 1]
                r = turn - jnp.round(turn)
                term = (lengths[d] * (r * horner(SIN_HALF, r * r))) ** 2
                total = term if total is None else total + term
            squares.append(total)
        short = None
        for n in range(mix_ref.shape[0]):
            rate = rate_ref[n]
            ahead, behind = [], []
            for t in range(slots):
                rows = slice((b + t) * BLOCK, (b + t + 1) * BLOCK)
                weight = jnp.exp(-rate * squares[t])
                ahead.append(weight * row_ref[8 + t : 9 + t, mine])
                behind.append(weight * col_ref[rows, 8 + slots - 1 - t : 8 + slots - t])
            gathered = dot3([x[:, around] for x in near], split(jnp.concatenate(ahead, axis=0)), NN)
            returned = dot3([x[:, around] for x in far], split(jnp.concatenate(behind, axis=0)), NN)
            mix = split(mix_ref[n])
            forth = dot3(mix, split(gathered), TN)
            back = dot3(mix, split(returned), NN)
            short = (forth, back) if short is None else (short[0] + forth, short[1] + back)
        short_ref[:, mine] = short[0]
        back_ref[:, mine] = short[1]


def short_call(near, far, col, row, radial_mix, radial_rates, total_blocks):
    channels, own = near.shape[0], row.shape[1]
    vmem = pl.BlockSpec(memory_space=pltpu.VMEM)
    return pl.pallas_call(
        functools.partial(short_kernel, total_blocks),
        out_shape=(jax.ShapeDtypeStruct((channels, own), jnp.float32),) * 2,
        in_specs=[vmem] * 5 + [pl.BlockSpec(memory_space=pltpu.SMEM)],
        out_specs=[vmem] * 2,
        compiler_params=pltpu.CompilerParams(vmem_limit_bytes=VMEM_LIMIT),
        cost_estimate=pl.CostEstimate(flops=6_000_000_000, bytes_accessed=4_000_000, transcendentals=0),
        name="short_range",
    )(near, far, col, row, radial_mix, radial_rates)


def per_device(features, positions, wavevectors, mode_filter, radial_mix, radial_rates, neighbour_ids, live_counts, cotangent):
    channels, shard_atoms = features.shape
    atom_devices = lax.axis_size("atom")
    mode_devices = lax.axis_size("mode")
    total_atoms = shard_atoms * atom_devices
    inverse_count = 1.0 / total_atoms
    total_blocks = total_atoms // BLOCK
    owned_blocks = neighbour_ids.shape[0]
    owned_rows = owned_blocks * BLOCK
    reach_rows = REACH * BLOCK
    mode_index = lax.axis_index("mode")
    atom_index = lax.axis_index("atom")

    first_own = (atom_index * mode_devices + mode_index) * owned_blocks
    offsets = jnp.mod(
        neighbour_ids - (first_own + jnp.arange(owned_blocks, dtype=jnp.int32))[:, None] + REACH, total_blocks
    )
    live = jnp.arange(SLOTS, dtype=jnp.int32)[None, :] < live_counts[:, None]
    masks = jnp.sum(
        jnp.where(live[:, :, None] & (offsets[:, :, None] == jnp.arange(8, dtype=jnp.int32)), 1.0, 0.0), axis=1
    )
    mask_rows = jnp.repeat(masks.T, BLOCK, axis=1)
    mine = mode_index * owned_rows
    own_feat = lax.dynamic_slice_in_dim(features, mine, owned_rows, 1)
    own_pos = lax.dynamic_slice_in_dim(positions, mine, owned_rows, 1)
    stacked = jnp.concatenate([own_feat, cotangent, jnp.pad(own_pos, ((0, 5), (0, 0))), mask_rows], axis=0)
    devices = atom_devices * mode_devices
    steps = -(-reach_rows // owned_rows)
    shift = lambda k: lax.ppermute(stacked, ("atom", "mode"), [(i, (i + k) % devices) for i in range(devices)])
    around = [shift(k) for k in range(steps, 0, -1)] + [stacked] + [shift(-k) for k in range(1, steps + 1)]

    waves = wavevectors.astype(jnp.float32).T
    width = mode_filter.shape[1] // atom_devices
    cut = width % 128 != 0
    filters = mode_filter.reshape(channels, atom_devices, width).transpose(1, 0, 2) if cut else mode_filter
    parts, grad_filter = spectral_call(
        features, cotangent, positions, waves, filters, atom_devices, mode_devices, inverse_count
    )
    if cut:
        grad_filter = grad_filter.transpose(1, 0, 2).reshape(channels, -1)

    spare = steps * owned_rows - reach_rows
    window = jnp.concatenate(around, axis=1)[:, spare : spare + owned_rows + 2 * reach_rows]
    small = window[2 * channels :]
    short_own, back_short = short_call(
        window[:channels],
        window[channels : 2 * channels],
        small.T,
        small[:, reach_rows:-reach_rows],
        radial_mix,
        radial_rates,
        total_blocks,
    )

    own = lax.dynamic_index_in_dim(parts, mode_index, 0, keepdims=False)
    for r in range(1, mode_devices):
        chunk = lax.dynamic_index_in_dim(parts, (mode_index + r) % mode_devices, 0, keepdims=False)
        own = own + lax.ppermute(chunk, "mode", [(i, (i + r) % mode_devices) for i in range(mode_devices)])
    half = channels // 2
    return (
        own_feat + jnp.concatenate([own[:half], own[channels : channels + half]], axis=0) + short_own,
        cotangent + jnp.concatenate([own[half:channels], own[channels + half :]], axis=0) + back_short,
        grad_filter,
    )


def solution(mesh):
    in_specs = (
        P(None, "atom"),
        P(None, "atom"),
        P(None, "mode"),
        P(None, "mode"),
        P(),
        P(),
        P(("atom", "mode"), None),
        P(("atom", "mode")),
        P(None, ("atom", "mode")),
    )
    out_specs = (P(None, ("atom", "mode")), P(None, ("atom", "mode")), P(None, "mode"))
    return jax.shard_map(per_device, mesh=mesh, in_specs=in_specs, out_specs=out_specs, check_vma=False)
```

```python
import functools

import jax
import jax.numpy as jnp
from jax import lax
from jax.experimental import pallas as pl
from jax.experimental.pallas import tpu as pltpu
from jax.sharding import PartitionSpec as P

BLOCK = 128
REACH = 2
SLOTS = 5
ROWS = 16
VMEM_LIMIT = 56 * 1024 * 1024

SIN_ROOT = (4.442882919124344, -7.308245686508998, 3.606354218431858, -0.8461116503680876, 0.10982451641509068)
COS_ROOT = (1.4142134962552282, -6.978850948563766, 5.73946037690631, -1.8835579059813616, 0.31068802751622054)
SIN_HALF = (3.141592640130707, -5.167710083507862, 2.550077523214134, -0.5982912856178576, 0.0776576603009221)


def horner(coefs, z):
    value = coefs[-1]
    for coef in coefs[-2::-1]:
        value = value * z + coef
    return value


def split(x):
    high = x.astype(jnp.bfloat16)
    return high, (x - high.astype(jnp.float32)).astype(jnp.bfloat16)


def dot3(left, right, dims):
    def one(a, b):
        return lax.dot_general(a, b, (dims, ((), ())), preferred_element_type=jnp.float32)

    return one(left[0], right[0]) + (one(left[0], right[1]) + one(left[1], right[0]))


NN = ((1,), (0,))
NT = ((1,), (1,))
TN = ((0,), (0,))


def short_range(total_blocks, near, far, cols_ref, small, mix_ref, rate_ref, store):
    window = near[0].shape[1]
    own = small.shape[1]
    lengths = (total_blocks / jnp.pi, 2.0 / jnp.pi, 2.0 / jnp.pi)
    reach = window - own + BLOCK
    slots = reach // BLOCK
    base = cols_ref.shape[1] - 16
    for b in range(own // BLOCK):
        mine = slice(b * BLOCK, (b + 1) * BLOCK)
        around = slice(b * BLOCK, b * BLOCK + reach)
        squares = []
        for t in range(slots):
            rows = slice((b + t) * BLOCK, (b + t + 1) * BLOCK)
            total = None
            for d in range(3):
                turn = small[d : d + 1, mine] - cols_ref[rows, base + d : base + d + 1]
                r = turn - jnp.round(turn)
                term = (lengths[d] * (r * horner(SIN_HALF, r * r))) ** 2
                total = term if total is None else total + term
            squares.append(total)
        short = None
        for n in range(mix_ref.shape[0]):
            rate = rate_ref[n]
            ahead, behind = [], []
            for t in range(slots):
                rows = slice((b + t) * BLOCK, (b + t + 1) * BLOCK)
                at = base + 8 + slots - 1 - t
                weight = jnp.exp(-rate * squares[t])
                ahead.append(weight * small[8 + t : 9 + t, mine])
                behind.append(weight * cols_ref[rows, at : at + 1])
            gathered = dot3([x[:, around] for x in near], split(jnp.concatenate(ahead, axis=0)), NN)
            returned = dot3([x[:, around] for x in far], split(jnp.concatenate(behind, axis=0)), NN)
            mix = split(mix_ref[n])
            forth = dot3(mix, split(gathered), TN)
            back = dot3(mix, split(returned), NN)
            short = (forth, back) if short is None else (short[0] + forth, short[1] + back)
        store[0, :, mine] = short[0]
        store[1, :, mine] = short[1]


def bits_of(count):
    return [1 << k for k in range(count.bit_length() - 1)]


def layer_kernel(
    n, m, total_blocks, scale,
    feat_ref, cot_ref, pos_ref, wave_ref, filt_ref, mix_ref, rate_ref, ids_ref, live_ref,
    layer_ref, cotgrad_ref, grad_ref,
    mine, halo, nh, nl, xh, xl, cols_ref, shorts, out_ref, out_in,
    fh, fl, cots, ch, cl, sh, sl, held, pair_in, halves_in, full,
    h_send, h_recv, o_send, o_recv, z_send, z_recv, c_send, c_recv, r_send, r_recv, g_send, g_recv, k_send, k_recv,
):
    atom = lax.axis_index("atom")
    mode = lax.axis_index("mode")
    channels, atoms = feat_ref.shape
    part = channels // 2
    own = cot_ref.shape[1]
    tile = ch.shape[1]
    bits = bits_of(n)
    core, rest = bits[0], bits[1:]
    orders = (rest, rest[::-1])
    signs = {bit: 1 - 2 * ((atom // bit) % 2) for bit in bits}

    def at(e):
        place = atom
        for bit in bits:
            if e & bit:
                place = place + signs[bit] * bit
        return place

    def share_of(ref, e, h):
        rows = pl.ds(h * part, part)
        if len(ref.shape) == 3:
            return ref.at[at(e), rows, :]
        return ref.at[rows, pl.ds(pl.multiple_of(at(e) * tile, tile), tile)]

    def remote(src, dst, send, recv, where):
        return pltpu.make_async_remote_copy(
            src_ref=src, dst_ref=dst, send_sem=send, recv_sem=recv, device_id=where, device_id_type=pl.DeviceIdType.MESH
        )

    def along(k):
        target = lax.rem(atom * m + mode + k + n * m, n * m)
        return {"atom": target // m, "mode": lax.rem(target, m)}

    steps = -(-REACH * BLOCK // own)
    shifts = [k for k in range(-steps, steps + 1) if k]
    peers = [{"atom": at(bit)} for bit in bits] + [{"mode": lax.rem(mode + r, m)} for r in range(1, m)]
    peers += [along(k) for k in shifts]
    barrier = pltpu.get_barrier_semaphore()
    for peer in peers:
        pl.semaphore_signal(barrier, inc=1, device_id=peer, device_id_type=pl.DeviceIdType.MESH)
    pl.semaphore_wait(barrier, len(peers))

    gathers = []
    for r in range(1, m):
        gathers.append(remote(cot_ref, cots.at[r - 1], z_send.at[r - 1], z_recv.at[r - 1], {"mode": lax.rem(mode + r, m)}))
        gathers[-1].start()

    own_cols = pl.ds(pl.multiple_of(mode * own, own), own)
    mine[:channels, :] = feat_ref[:, own_cols]
    mine[channels : 2 * channels, :] = cot_ref[...]
    small_rows = 2 * channels
    mine[small_rows:, :] = jnp.zeros((16, own), jnp.float32)
    mine[small_rows : small_rows + 3, :] = pos_ref[:, own_cols]
    first_own = (atom * m + mode) * (own // BLOCK)
    for b in range(own // BLOCK):
        offsets = [lax.rem(ids_ref[b, t] - first_own - b + REACH + 2 * total_blocks, total_blocks) for t in range(SLOTS)]
        for o in range(SLOTS):
            value = jnp.float32(0.0)
            for t in range(SLOTS):
                value += jnp.where((offsets[t] == o) & (t < live_ref[b]), 1.0, 0.0)
            mine[small_rows + 8 + o : small_rows + 9 + o, b * BLOCK : (b + 1) * BLOCK] = jnp.full((1, BLOCK), value)
    halos = []
    for slot, k in enumerate(shifts):
        halos.append(remote(mine, halo.at[slot], h_send.at[slot], h_recv.at[slot], along(-k)))
        halos[-1].start()

    def neighbourhood():
        for copy in halos:
            copy.wait_recv()
        pieces = [halo[slot] for slot in range(steps)] + [mine[...]] + [halo[slot] for slot in range(steps, 2 * steps)]
        spare = steps * own - REACH * BLOCK
        width = own + 2 * REACH * BLOCK
        near = jnp.concatenate([x[:channels] for x in pieces], axis=1)[:, spare : spare + width]
        far = jnp.concatenate([x[channels : 2 * channels] for x in pieces], axis=1)[:, spare : spare + width]
        nh[...], nl[...] = split(near)
        xh[...], xl[...] = split(far)
        last = jnp.concatenate([x[small_rows + 16 - BLOCK :] for x in pieces], axis=1)[:, spare : spare + width]
        for b in range(width // BLOCK):
            part_cols = slice(b * BLOCK, (b + 1) * BLOCK)
            cols_ref[part_cols, :] = last[:, part_cols].T
        short_range(
            total_blocks, (nh, nl), (xh, xl), cols_ref, mine[small_rows:, :], mix_ref, rate_ref, shorts
        )

    def trig(e):
        first = at(e) * tile

        @pl.loop(0, tile // ROWS)
        def _(step):
            rows = pl.ds(pl.multiple_of(step * ROWS, ROWS), ROWS)
            wave = wave_ref[pl.ds(pl.multiple_of(first + step * ROWS, ROWS), ROWS), :]
            turns = (
                wave[:, 0:1] * pos_ref[0:1, :] + wave[:, 1:2] * pos_ref[1:2, :] + wave[:, 2:3] * pos_ref[2:3, :]
            )
            r = turns - jnp.round(turns)
            z = r * r
            s = r * horner(SIN_ROOT, z)
            c = horner(COS_ROOT, z)
            ch[e, rows, :], cl[e, rows, :] = split(1.0 - s * s)
            sh[e, rows, :], sl[e, rows, :] = split(s * c)

    def place(rows_from, value, cols):
        high, low = split(value)
        for h in range(2):
            rows = slice(h * channels + rows_from, h * channels + rows_from + part)
            fh[rows, cols] = high[h * part : (h + 1) * part]
            fl[rows, cols] = low[h * part : (h + 1) * part]

    place(0, feat_ref[...], slice(None))
    place(part, cot_ref[...], pl.ds(pl.multiple_of(mode * own, own), own))

    evens = [e for e in range(n - 2, -1, -2)]
    sequence = [t for e in evens for t in (e + 1, e)]
    ahead = n // 2
    for e in sequence[:ahead]:
        trig(e)
    for r in range(1, m):
        gathers[r - 1].wait_recv()
        sender = lax.rem(mode - r + m, m)
        place(part, cots[r - 1], pl.ds(pl.multiple_of(sender * own, own), own))

    sent = gathers + halos

    def sums(e):
        left = (fh[...], fl[...])
        for k, (high, low) in enumerate(((ch, cl), (sh, sl))):
            result = dot3(left, (high[e], low[e]), NT)
            held[e, 0, k] = result[:channels]
            held[e, 1, k] = result[channels:]

    landing = {}
    for h in range(2):
        live = evens
        for s, bit in enumerate(orders[h]):
            for e in live:
                if not e & bit:
                    landing[h, s, e] = len(landing)
            live = [e for e in live if not e & bit]

    def stage_copy(h, s, e):
        bit = orders[h][s]
        slot = landing[h, s, e & ~bit]
        return remote(held.at[e | bit, h], halves_in.at[slot], r_send.at[slot], r_recv.at[slot], {"atom": at(bit)})

    def advance(h, e):
        for s, bit in enumerate(orders[h]):
            copy = stage_copy(h, s, e)
            if e & bit:
                copy.start()
                sent.append(copy)
                return
            copy.wait_recv()
            held[e, h] += halves_in[landing[h, s, e]]

    for number, e in enumerate(evens):
        if 2 * number >= ahead:
            trig(e + 1)
        sums(e + 1)
        across = remote(held.at[e + 1], pair_in.at[e // 2], c_send.at[e // 2], c_recv.at[e // 2], {"atom": at(core)})
        across.start()
        sent.append(across)
        if 2 * number + 1 >= ahead:
            trig(e)
        sums(e)
        across.wait_recv()
        held[e] += pair_in[e // 2]
        for h in range(2):
            advance(h, e)

    back = [order[::-1] for order in orders]

    def box(h, e):
        return held.at[0, h] if e == 0 else full.at[e, h]

    def half_copy(h, e, bit):
        slot = h * n + (e | bit)
        return remote(box(h, e), full.at[e | bit, h], g_send.at[slot], g_recv.at[slot], {"atom": at(bit)})

    def last_of(h, e):
        return max(p for p, bit in enumerate(back[h]) if e & bit)

    def forward(h, e, first):
        for bit in back[h][first:]:
            copy = half_copy(h, e, bit)
            copy.start()
            sent.append(copy)

    def core_copy(e):
        source = held.at[0] if e == 0 else full.at[e]
        return remote(source, full.at[e | core], k_send.at[e // 2], k_recv.at[e // 2], {"atom": at(core)})

    def arrive(h, e):
        p = last_of(h, e)
        half_copy(h, e & ~back[h][p], back[h][p]).wait_recv()
        forward(h, e, p + 1)

    def give_back(e, first):
        value = held if e == 0 else full
        left = []
        for k in range(2):
            rows = []
            for h in range(2):
                factor = share_of(filt_ref, e, h)[...] * scale
                rows += [factor * value[e, h, k, :part], factor * value[e, h, k, part:]]
            left.append(split(jnp.concatenate(rows, axis=0)))
        for h in range(2):
            share_of(grad_ref, e, h)[...] = (
                value[e, h, 0, :part] * value[e, h, 0, part:] + value[e, h, 1, :part] * value[e, h, 1, part:]
            ) * scale
        for q in range(m):
            chunk = slice(q * own, (q + 1) * own)
            total = dot3(left[0], (ch[e, :, chunk], cl[e, :, chunk]), NN) + dot3(
                left[1], (sh[e, :, chunk], sl[e, :, chunk]), NN
            )
            if first:
                out_ref[q] = total
            else:
                out_ref[q] += total

    for stage in range(len(rest)):
        for h in range(2):
            copy = half_copy(h, 0, back[h][stage])
            copy.start()
            sent.append(copy)
    copy = core_copy(0)
    copy.start()
    sent.append(copy)
    give_back(0, True)
    neighbourhood()

    arrivals = sorted(
        ((h, e) for e in evens if e for h in range(2)), key=lambda x: (bin(x[1]).count("1"), last_of(*x), x[1])
    )
    waiting = 0
    arrived = set()
    for h, e in arrivals:
        arrive(h, e)
        arrived.add((h, e))
        if (1 - h, e) in arrived:
            copy = core_copy(e)
            copy.start()
            sent.append(copy)
            core_copy(waiting).wait_recv()
            give_back(waiting | core, False)
            give_back(e, False)
            waiting = e
    core_copy(waiting).wait_recv()
    give_back(waiting | core, False)
    chunks = []
    for r in range(1, m):
        target = lax.rem(mode + r, m)
        chunks.append(remote(out_ref.at[target], out_in.at[r - 1], o_send.at[r - 1], o_recv.at[r - 1], {"mode": target}))
        chunks[-1].start()
    for copy in chunks:
        copy.wait_recv()
    for h in range(2):
        rows = slice(h * part, (h + 1) * part)
        for ref, k in ((layer_ref, 0), (cotgrad_ref, 1)):
            block = slice(h * channels + k * part, h * channels + (k + 1) * part)
            total = out_ref[mode, block, :]
            for r in range(1, m):
                total = total + out_in[r - 1, block, :]
            start = k * channels + h * part
            ref[rows, :] = mine[start : start + part, :] + total + shorts[k, rows, :]
    for copy in sent + chunks:
        copy.wait_send()


def layer_call(features, cotangent, positions, waves, filters, radial_mix, radial_rates, ids, live, n, m):
    channels, atoms = features.shape
    modes = waves.shape[0]
    tile = modes // n
    own = cotangent.shape[1]
    steps = -(-REACH * BLOCK // own)
    window = own + 2 * REACH * BLOCK
    rows = 2 * channels + 16
    vmem = pl.BlockSpec(memory_space=pltpu.VMEM)
    smem = pl.BlockSpec(memory_space=pltpu.SMEM)
    dma = pltpu.SemaphoreType.DMA
    f32 = lambda *shape: pltpu.VMEM(shape, jnp.float32)
    b16 = lambda *shape: pltpu.VMEM(shape, jnp.bfloat16)
    slots = 2 * (n // 2 - 1)
    pair = lambda count: [dma((count,)), dma((count,))]
    return pl.pallas_call(
        functools.partial(layer_kernel, n, m, n * atoms // BLOCK, 1.0 / (n * atoms)),
        out_shape=(
            jax.ShapeDtypeStruct((channels, own), jnp.float32),
            jax.ShapeDtypeStruct((channels, own), jnp.float32),
            jax.ShapeDtypeStruct(filters.shape, jnp.float32),
        ),
        in_specs=[vmem] * 6 + [smem] * 3,
        out_specs=[vmem] * 3,
        scratch_shapes=[
            f32(rows, own), f32(2 * steps, rows, own),
            b16(channels, window), b16(channels, window), b16(channels, window), b16(channels, window),
            f32(window, BLOCK), f32(2, channels, own),
            f32(m, 2 * channels, own), f32(m - 1, 2 * channels, own),
            b16(2 * channels, atoms), b16(2 * channels, atoms), f32(m - 1, channels, own),
            b16(n, tile, atoms), b16(n, tile, atoms), b16(n, tile, atoms), b16(n, tile, atoms),
            f32(n, 2, 2, channels, tile), f32(n // 2, 2, 2, channels, tile),
            f32(slots, 2, channels, tile), f32(n, 2, 2, channels, tile),
        ]
        + pair(2 * steps) + pair(m - 1) + pair(m - 1) + pair(n // 2) + pair(slots) + pair(2 * n) + pair(n // 2),
        compiler_params=pltpu.CompilerParams(vmem_limit_bytes=VMEM_LIMIT, collective_id=0, has_side_effects=True),
        name="layer",
    )(features, cotangent, positions, waves, filters, radial_mix, radial_rates, ids, live)


def per_device(features, positions, wavevectors, mode_filter, radial_mix, radial_rates, neighbour_ids, live_counts, cotangent):
    channels = features.shape[0]
    n = lax.axis_size("atom")
    m = lax.axis_size("mode")
    waves = wavevectors.astype(jnp.float32).T
    width = mode_filter.shape[1] // n
    cut = width % 128 != 0
    filters = mode_filter.reshape(channels, n, width).transpose(1, 0, 2) if cut else mode_filter
    layer_out, grad_features, grad_filter = layer_call(
        features, cotangent, positions, waves, filters, radial_mix, radial_rates, neighbour_ids, live_counts, n, m
    )
    if cut:
        grad_filter = grad_filter.transpose(1, 0, 2).reshape(channels, -1)
    return layer_out, grad_features, grad_filter


def solution(mesh):
    in_specs = (
        P(None, "atom"),
        P(None, "atom"),
        P(None, "mode"),
        P(None, "mode"),
        P(),
        P(),
        P(("atom", "mode"), None),
        P(("atom", "mode")),
        P(None, ("atom", "mode")),
    )
    out_specs = (P(None, ("atom", "mode")), P(None, ("atom", "mode")), P(None, "mode"))
    return jax.shard_map(per_device, mesh=mesh, in_specs=in_specs, out_specs=out_specs, check_vma=False)
```

```python
import functools

import jax
import jax.numpy as jnp
from jax import lax
from jax.experimental import pallas as pl
from jax.experimental.pallas import tpu as pltpu
from jax.sharding import PartitionSpec as P

BLOCK = 128
REACH = 2
SLOTS = 5
ROWS = 16
VMEM_LIMIT = 56 * 1024 * 1024

SIN_ROOT = (4.442882919124344, -7.308245686508998, 3.606354218431858, -0.8461116503680876, 0.10982451641509068)
COS_ROOT = (1.4142134962552282, -6.978850948563766, 5.73946037690631, -1.8835579059813616, 0.31068802751622054)
SIN_HALF = (3.141592640130707, -5.167710083507862, 2.550077523214134, -0.5982912856178576, 0.0776576603009221)


def horner(coefs, z):
    value = coefs[-1]
    for coef in coefs[-2::-1]:
        value = value * z + coef
    return value


def split(x):
    high = x.astype(jnp.bfloat16)
    return high, (x - high.astype(jnp.float32)).astype(jnp.bfloat16)


def dot3(left, right, dims):
    def one(a, b):
        return lax.dot_general(a, b, (dims, ((), ())), preferred_element_type=jnp.float32)

    return one(left[0], right[0]) + (one(left[0], right[1]) + one(left[1], right[0]))


NN = ((1,), (0,))
NT = ((1,), (1,))
TN = ((0,), (0,))


def short_range(total_blocks, near, far, cols_ref, small, mix_ref, rate_ref, store):
    window = near[0].shape[1]
    own = small.shape[1]
    lengths = (total_blocks / jnp.pi, 2.0 / jnp.pi, 2.0 / jnp.pi)
    reach = window - own + BLOCK
    slots = reach // BLOCK
    base = cols_ref.shape[1] - 16
    for b in range(own // BLOCK):
        mine = slice(b * BLOCK, (b + 1) * BLOCK)
        around = slice(b * BLOCK, b * BLOCK + reach)
        squares = []
        for t in range(slots):
            rows = slice((b + t) * BLOCK, (b + t + 1) * BLOCK)
            total = None
            for d in range(3):
                turn = small[d : d + 1, mine] - cols_ref[rows, base + d : base + d + 1]
                r = turn - jnp.round(turn)
                term = (lengths[d] * (r * horner(SIN_HALF, r * r))) ** 2
                total = term if total is None else total + term
            squares.append(total)
        short = None
        for n in range(mix_ref.shape[0]):
            rate = rate_ref[n]
            ahead, behind = [], []
            for t in range(slots):
                rows = slice((b + t) * BLOCK, (b + t + 1) * BLOCK)
                at = base + 8 + slots - 1 - t
                weight = jnp.exp(-rate * squares[t])
                ahead.append(weight * small[8 + t : 9 + t, mine])
                behind.append(weight * cols_ref[rows, at : at + 1])
            gathered = dot3([x[:, around] for x in near], split(jnp.concatenate(ahead, axis=0)), NN)
            returned = dot3([x[:, around] for x in far], split(jnp.concatenate(behind, axis=0)), NN)
            mix = split(mix_ref[n])
            forth = dot3(mix, split(gathered), TN)
            back = dot3(mix, split(returned), NN)
            short = (forth, back) if short is None else (short[0] + forth, short[1] + back)
        store[0, :, mine] = short[0]
        store[1, :, mine] = short[1]


def bits_of(count):
    return [1 << k for k in range(count.bit_length() - 1)]


def layer_kernel(
    n, m, total_blocks, scale,
    feat_ref, cot_ref, pos_ref, wave_ref, filt_ref, mix_ref, rate_ref, ids_ref, live_ref,
    layer_ref, cotgrad_ref, grad_ref,
    mine, halo, nh, nl, xh, xl, cols_ref, shorts, out_ref, out_in,
    fh, fl, cots, ch, cl, sh, sl, held, pair_in, halves_in, full,
    h_send, h_recv, o_send, o_recv, z_send, z_recv, c_send, c_recv, r_send, r_recv, g_send, g_recv, k_send, k_recv,
):
    atom = lax.axis_index("atom")
    mode = lax.axis_index("mode")
    channels, atoms = feat_ref.shape
    part = channels // 2
    own = cot_ref.shape[1]
    tile = ch.shape[1]
    bits = bits_of(n)
    core, rest = bits[0], bits[1:]
    orders = (rest, rest[::-1])
    signs = {bit: 1 - 2 * ((atom // bit) % 2) for bit in bits}

    def at(e):
        place = atom
        for bit in bits:
            if e & bit:
                place = place + signs[bit] * bit
        return place

    def share_of(ref, e, h):
        rows = pl.ds(h * part, part)
        if len(ref.shape) == 3:
            return ref.at[at(e), rows, :]
        return ref.at[rows, pl.ds(pl.multiple_of(at(e) * tile, tile), tile)]

    def remote(src, dst, send, recv, where):
        return pltpu.make_async_remote_copy(
            src_ref=src, dst_ref=dst, send_sem=send, recv_sem=recv, device_id=where, device_id_type=pl.DeviceIdType.MESH
        )

    def along(k):
        target = lax.rem(atom * m + mode + k + n * m, n * m)
        return {"atom": target // m, "mode": lax.rem(target, m)}

    steps = -(-REACH * BLOCK // own)
    shifts = [k for k in range(-steps, steps + 1) if k]
    peers = [{"atom": at(bit)} for bit in bits] + [{"mode": lax.rem(mode + r, m)} for r in range(1, m)]
    peers += [along(k) for k in shifts]
    barrier = pltpu.get_barrier_semaphore()
    for peer in peers:
        pl.semaphore_signal(barrier, inc=1, device_id=peer, device_id_type=pl.DeviceIdType.MESH)
    pl.semaphore_wait(barrier, len(peers))

    gathers = []
    for r in range(1, m):
        gathers.append(remote(cot_ref, cots.at[r - 1], z_send.at[r - 1], z_recv.at[r - 1], {"mode": lax.rem(mode + r, m)}))
        gathers[-1].start()

    own_cols = pl.ds(pl.multiple_of(mode * own, own), own)
    mine[:channels, :] = feat_ref[:, own_cols]
    mine[channels : 2 * channels, :] = cot_ref[...]
    small_rows = 2 * channels
    mine[small_rows:, :] = jnp.zeros((16, own), jnp.float32)
    mine[small_rows : small_rows + 3, :] = pos_ref[:, own_cols]
    first_own = (atom * m + mode) * (own // BLOCK)
    for b in range(own // BLOCK):
        offsets = [lax.rem(ids_ref[b, t] - first_own - b + REACH + 2 * total_blocks, total_blocks) for t in range(SLOTS)]
        for o in range(SLOTS):
            value = jnp.float32(0.0)
            for t in range(SLOTS):
                value += jnp.where((offsets[t] == o) & (t < live_ref[b]), 1.0, 0.0)
            mine[small_rows + 8 + o : small_rows + 9 + o, b * BLOCK : (b + 1) * BLOCK] = jnp.full((1, BLOCK), value)
    halos = [
        remote(mine, halo.at[slot], h_send.at[slot], h_recv.at[slot], along(-k)) for slot, k in enumerate(shifts)
    ]

    def neighbourhood():
        for copy in halos:
            copy.wait_recv()
        pieces = [halo[slot] for slot in range(steps)] + [mine[...]] + [halo[slot] for slot in range(steps, 2 * steps)]
        spare = steps * own - REACH * BLOCK
        width = own + 2 * REACH * BLOCK
        near = jnp.concatenate([x[:channels] for x in pieces], axis=1)[:, spare : spare + width]
        far = jnp.concatenate([x[channels : 2 * channels] for x in pieces], axis=1)[:, spare : spare + width]
        nh[...], nl[...] = split(near)
        xh[...], xl[...] = split(far)
        last = jnp.concatenate([x[small_rows + 16 - BLOCK :] for x in pieces], axis=1)[:, spare : spare + width]
        for b in range(width // BLOCK):
            part_cols = slice(b * BLOCK, (b + 1) * BLOCK)
            cols_ref[part_cols, :] = last[:, part_cols].T
        short_range(
            total_blocks, (nh, nl), (xh, xl), cols_ref, mine[small_rows:, :], mix_ref, rate_ref, shorts
        )

    def trig_rows(e, first, step):
        rows = pl.ds(pl.multiple_of(step * ROWS, ROWS), ROWS)
        wave = wave_ref[pl.ds(pl.multiple_of(first + step * ROWS, ROWS), ROWS), :]
        turns = (
            wave[:, 0:1] * pos_ref[0:1, :] + wave[:, 1:2] * pos_ref[1:2, :] + wave[:, 2:3] * pos_ref[2:3, :]
        )
        r = turns - jnp.round(turns)
        z = r * r
        s = r * horner(SIN_ROOT, z)
        c = horner(COS_ROOT, z)
        ch[e, rows, :], cl[e, rows, :] = split(1.0 - s * s)
        sh[e, rows, :], sl[e, rows, :] = split(s * c)

    def trig(e):
        first = at(e) * tile

        @pl.loop(0, tile // ROWS)
        def _(step):
            trig_rows(e, first, step)

    def sums_and_trig(e, following):
        slices = 4
        depth = atoms // slices
        count = tile // ROWS // slices
        first = at(following) * tile
        for k in range(2):
            held[e, 0, k] = jnp.zeros((channels, tile), jnp.float32)
            held[e, 1, k] = jnp.zeros((channels, tile), jnp.float32)

        @pl.loop(0, slices)
        def _(j):
            cols = pl.ds(pl.multiple_of(j * depth, depth), depth)
            left = (fh[:, cols], fl[:, cols])
            for k, (high, low) in enumerate(((ch, cl), (sh, sl))):
                result = dot3(left, (high[e, :, cols], low[e, :, cols]), NT)
                held[e, 0, k] += result[:channels]
                held[e, 1, k] += result[channels:]
                for i in range(k * count // 2, (k + 1) * count // 2):
                    trig_rows(following, first, j * count + i)

    def place(rows_from, value, cols):
        high, low = split(value)
        for h in range(2):
            rows = slice(h * channels + rows_from, h * channels + rows_from + part)
            fh[rows, cols] = high[h * part : (h + 1) * part]
            fl[rows, cols] = low[h * part : (h + 1) * part]

    place(0, feat_ref[...], slice(None))
    place(part, cot_ref[...], pl.ds(pl.multiple_of(mode * own, own), own))

    evens = [e for e in range(n - 2, -1, -2)]
    sequence = [t for e in evens for t in (e + 1, e)]
    ahead = n // 2
    for e in sequence[:ahead]:
        trig(e)
    for r in range(1, m):
        gathers[r - 1].wait_recv()
        sender = lax.rem(mode - r + m, m)
        place(part, cots[r - 1], pl.ds(pl.multiple_of(sender * own, own), own))

    for copy in halos:
        copy.start()
    sent = gathers + halos

    def sums(e):
        left = (fh[...], fl[...])
        for k, (high, low) in enumerate(((ch, cl), (sh, sl))):
            result = dot3(left, (high[e], low[e]), NT)
            held[e, 0, k] = result[:channels]
            held[e, 1, k] = result[channels:]

    landing = {}
    for h in range(2):
        live = evens
        for s, bit in enumerate(orders[h]):
            for e in live:
                if not e & bit:
                    landing[h, s, e] = len(landing)
            live = [e for e in live if not e & bit]

    def stage_copy(h, s, e):
        bit = orders[h][s]
        slot = landing[h, s, e & ~bit]
        return remote(held.at[e | bit, h], halves_in.at[slot], r_send.at[slot], r_recv.at[slot], {"atom": at(bit)})

    def advance(h, e):
        for s, bit in enumerate(orders[h]):
            copy = stage_copy(h, s, e)
            if e & bit:
                copy.start()
                sent.append(copy)
                return
            copy.wait_recv()
            held[e, h] += halves_in[landing[h, s, e]]

    def step_of(number):
        e, following = sequence[number], number + ahead
        if following < n:
            sums_and_trig(e, sequence[following])
        else:
            sums(e)

    for number, e in enumerate(evens):
        step_of(2 * number)
        across = remote(held.at[e + 1], pair_in.at[e // 2], c_send.at[e // 2], c_recv.at[e // 2], {"atom": at(core)})
        across.start()
        sent.append(across)
        step_of(2 * number + 1)
        across.wait_recv()
        held[e] += pair_in[e // 2]
        for h in range(2):
            advance(h, e)

    back = [order[::-1] for order in orders]

    def box(h, e):
        return held.at[0, h] if e == 0 else full.at[e, h]

    def half_copy(h, e, bit):
        slot = h * n + (e | bit)
        return remote(box(h, e), full.at[e | bit, h], g_send.at[slot], g_recv.at[slot], {"atom": at(bit)})

    def last_of(h, e):
        return max(p for p, bit in enumerate(back[h]) if e & bit)

    def forward(h, e, first):
        for bit in back[h][first:]:
            copy = half_copy(h, e, bit)
            copy.start()
            sent.append(copy)

    def core_copy(e):
        source = held.at[0] if e == 0 else full.at[e]
        return remote(source, full.at[e | core], k_send.at[e // 2], k_recv.at[e // 2], {"atom": at(core)})

    def arrive(h, e):
        p = last_of(h, e)
        half_copy(h, e & ~back[h][p], back[h][p]).wait_recv()
        forward(h, e, p + 1)

    def give_back(e, first):
        value = held if e == 0 else full
        left = []
        for k in range(2):
            rows = []
            for h in range(2):
                factor = share_of(filt_ref, e, h)[...] * scale
                rows += [factor * value[e, h, k, :part], factor * value[e, h, k, part:]]
            left.append(split(jnp.concatenate(rows, axis=0)))
        for h in range(2):
            share_of(grad_ref, e, h)[...] = (
                value[e, h, 0, :part] * value[e, h, 0, part:] + value[e, h, 1, :part] * value[e, h, 1, part:]
            ) * scale
        for q in range(m):
            chunk = slice(q * own, (q + 1) * own)
            total = dot3(left[0], (ch[e, :, chunk], cl[e, :, chunk]), NN) + dot3(
                left[1], (sh[e, :, chunk], sl[e, :, chunk]), NN
            )
            if first:
                out_ref[q] = total
            else:
                out_ref[q] += total

    for stage in range(len(rest)):
        for h in range(2):
            copy = half_copy(h, 0, back[h][stage])
            copy.start()
            sent.append(copy)
    copy = core_copy(0)
    copy.start()
    sent.append(copy)
    give_back(0, True)

    arrivals = sorted(
        ((h, e) for e in evens if e for h in range(2)), key=lambda x: (bin(x[1]).count("1"), last_of(*x), x[1])
    )
    waiting = 0
    arrived = set()
    for h, e in arrivals:
        arrive(h, e)
        arrived.add((h, e))
        if (1 - h, e) in arrived:
            copy = core_copy(e)
            copy.start()
            sent.append(copy)
            core_copy(waiting).wait_recv()
            give_back(waiting | core, False)
            give_back(e, False)
            waiting = e
    core_copy(waiting).wait_recv()
    give_back(waiting | core, False)
    chunks = []
    for r in range(1, m):
        target = lax.rem(mode + r, m)
        chunks.append(remote(out_ref.at[target], out_in.at[r - 1], o_send.at[r - 1], o_recv.at[r - 1], {"mode": target}))
        chunks[-1].start()
    neighbourhood()
    for copy in chunks:
        copy.wait_recv()
    for h in range(2):
        rows = slice(h * part, (h + 1) * part)
        for ref, k in ((layer_ref, 0), (cotgrad_ref, 1)):
            block = slice(h * channels + k * part, h * channels + (k + 1) * part)
            total = out_ref[mode, block, :]
            for r in range(1, m):
                total = total + out_in[r - 1, block, :]
            start = k * channels + h * part
            ref[rows, :] = mine[start : start + part, :] + total + shorts[k, rows, :]
    for copy in sent + chunks:
        copy.wait_send()


def layer_call(features, cotangent, positions, waves, filters, radial_mix, radial_rates, ids, live, n, m):
    channels, atoms = features.shape
    modes = waves.shape[0]
    tile = modes // n
    own = cotangent.shape[1]
    steps = -(-REACH * BLOCK // own)
    window = own + 2 * REACH * BLOCK
    rows = 2 * channels + 16
    vmem = pl.BlockSpec(memory_space=pltpu.VMEM)
    smem = pl.BlockSpec(memory_space=pltpu.SMEM)
    dma = pltpu.SemaphoreType.DMA
    f32 = lambda *shape: pltpu.VMEM(shape, jnp.float32)
    b16 = lambda *shape: pltpu.VMEM(shape, jnp.bfloat16)
    slots = 2 * (n // 2 - 1)
    pair = lambda count: [dma((count,)), dma((count,))]
    return pl.pallas_call(
        functools.partial(layer_kernel, n, m, n * atoms // BLOCK, 1.0 / (n * atoms)),
        out_shape=(
            jax.ShapeDtypeStruct((channels, own), jnp.float32),
            jax.ShapeDtypeStruct((channels, own), jnp.float32),
            jax.ShapeDtypeStruct(filters.shape, jnp.float32),
        ),
        in_specs=[vmem] * 6 + [smem] * 3,
        out_specs=[vmem] * 3,
        scratch_shapes=[
            f32(rows, own), f32(2 * steps, rows, own),
            b16(channels, window), b16(channels, window), b16(channels, window), b16(channels, window),
            f32(window, BLOCK), f32(2, channels, own),
            f32(m, 2 * channels, own), f32(m - 1, 2 * channels, own),
            b16(2 * channels, atoms), b16(2 * channels, atoms), f32(m - 1, channels, own),
            b16(n, tile, atoms), b16(n, tile, atoms), b16(n, tile, atoms), b16(n, tile, atoms),
            f32(n, 2, 2, channels, tile), f32(n // 2, 2, 2, channels, tile),
            f32(slots, 2, channels, tile), f32(n, 2, 2, channels, tile),
        ]
        + pair(2 * steps) + pair(m - 1) + pair(m - 1) + pair(n // 2) + pair(slots) + pair(2 * n) + pair(n // 2),
        compiler_params=pltpu.CompilerParams(vmem_limit_bytes=VMEM_LIMIT, collective_id=0, has_side_effects=True),
        name="layer",
    )(features, cotangent, positions, waves, filters, radial_mix, radial_rates, ids, live)


def per_device(features, positions, wavevectors, mode_filter, radial_mix, radial_rates, neighbour_ids, live_counts, cotangent):
    channels = features.shape[0]
    n = lax.axis_size("atom")
    m = lax.axis_size("mode")
    waves = wavevectors.astype(jnp.float32).T
    width = mode_filter.shape[1] // n
    cut = width % 128 != 0
    filters = mode_filter.reshape(channels, n, width).transpose(1, 0, 2) if cut else mode_filter
    layer_out, grad_features, grad_filter = layer_call(
        features, cotangent, positions, waves, filters, radial_mix, radial_rates, neighbour_ids, live_counts, n, m
    )
    if cut:
        grad_filter = grad_filter.transpose(1, 0, 2).reshape(channels, -1)
    return layer_out, grad_features, grad_filter


def solution(mesh):
    in_specs = (
        P(None, "atom"),
        P(None, "atom"),
        P(None, "mode"),
        P(None, "mode"),
        P(),
        P(),
        P(("atom", "mode"), None),
        P(("atom", "mode")),
        P(None, ("atom", "mode")),
    )
    out_specs = (P(None, ("atom", "mode")), P(None, ("atom", "mode")), P(None, "mode"))
    return jax.shard_map(per_device, mesh=mesh, in_specs=in_specs, out_specs=out_specs, check_vma=False)
```
